512 devices in a mesh: recv: 32 (over x, z_lo, core), src: 16 (over y, z_hi).
Axes of the slice: x: 4, y: 8, z: 8 (z_hi: 2, z_lo: 4; z = z_hi * 4 + z_lo), core: 2. Of those that a mesh axis runs over, the one named last changes fastest.
Arguments:
- record: bfloat16 [512, 131072], P('recv', 'src'), may hold values from -41 to 41
- source_channel: int32 [32], replicated, may hold values from 0 to 511, as said below
- band_edges: int32 [32, 2], replicated, may hold values from 0 to 512, as said below
- offsets: int32 [16], replicated, may hold values from 0 to 5376, as said below
Outputs:
- virtual_gathers: float32 [32, 512, 256], P('src', 'recv')
The draws below stay inside these ranges and needn't reach their ends.
Inputs may be any that keep to these rules, and one draw needn't show every extreme that they name: `source_channel`: the 32 channels are distinct. band_edges[s, 0] < band_edges[s, 1] for every source. `offsets`: window w lies inside time shard w.
All inputs are finite; a program needn't handle non-finite values.
Results may differ from the reference program's by a relative error of at most 0.0041.
Values may be sent and summed in bfloat16 or wider, within the bound.
No kernel may reach another device: no remote copies, remote signals or barrier semaphores. Data moves between devices by JAX's collectives and lax.ppermute only.
A program may use at most 64 MiB of HBM per device.

```python
import jax
import jax.numpy as jnp
from jax import lax

S = 32
WL = 2560
L = 256
T_DEV = 8192
SENSOR_COUNT = 512
TRACE_LENGTH = 131072
NW = 16
N_SRC = 16


def draw_record(key, part):
    divided_seeds = jax.random.split(key, 3)
    strain_readings = jnp.clip(jax.random.normal(divided_seeds[0], (SENSOR_COUNT, TRACE_LENGTH), jnp.float32), -6.0, 6.0)
    trace_magnitude = jnp.exp(jax.random.uniform(divided_seeds[1], (SENSOR_COUNT, 1), jnp.float32, -1.2, 1.2))
    random_transients = jnp.exp(jax.random.uniform(divided_seeds[2], (SENSOR_COUNT, TRACE_LENGTH // 64, 1), jnp.float32, -0.7, 0.7))
    folded_trace_matrix = (strain_readings.reshape(SENSOR_COUNT, TRACE_LENGTH // 64, 64) * random_transients).reshape(SENSOR_COUNT, TRACE_LENGTH) * trace_magnitude
    return folded_trace_matrix.astype(jnp.bfloat16)


def draw_source_channel(key, part):
    inner = jax.random.permutation(key, SENSOR_COUNT - 2)[:S - 2] + 1
    chosen = jnp.concatenate([jnp.zeros((1,), jnp.int32), inner.astype(jnp.int32), jnp.full((1,), SENSOR_COUNT - 1, jnp.int32)])
    order = jax.random.permutation(jax.random.fold_in(key, 1), S)
    return chosen[order].astype(jnp.int32)


def draw_band_edges(key, part):
    lower = jax.random.randint(key, (S,), 0, SENSOR_COUNT // 2)
    widths = jax.random.randint(jax.random.fold_in(key, 1), (S,), SENSOR_COUNT // 8, SENSOR_COUNT // 2 + 1)
    upper = lower + widths
    lower = lower.at[0].set(0)
    upper = upper.at[S - 1].set(SENSOR_COUNT)
    return jnp.stack([lower, upper], axis=1).astype(jnp.int32)


def draw_offsets(key, part):
    highest = T_DEV - WL - L
    values = jax.random.randint(key, (NW,), 0, highest + 1)
    values = values.at[0].set(0).at[NW - 1].set(highest)
    return values.astype(jnp.int32)


def setup_inputs(seed: int = 0) -> dict:
    key_list = jax.random.split(jax.random.key(seed), 5)
    return {
        "record": draw_record(jax.random.fold_in(key_list[4], 71), 0),
        "source_channel": draw_source_channel(jax.random.fold_in(key_list[4], 71), 0),
        "band_edges": draw_band_edges(jax.random.fold_in(key_list[4], 71), 0),
        "offsets": draw_offsets(jax.random.fold_in(key_list[4], 71), 0),
    }


EPSILON = 1e-06

def whiten(segment):
    values = segment.astype(jnp.float32)
    spread = jnp.sqrt(lax.optimization_barrier(jnp.mean(values * values, axis=-1, keepdims=True)) + EPSILON)
    return (values / spread).astype(jnp.bfloat16)

def reference(record, source_channel, band_edges, offsets):
    channels = record.shape[0]
    seg_len = WL + L
    channel_ids = jnp.arange(channels, dtype=jnp.int32)

    def one_window(running, window):
        window_start = (window * T_DEV + offsets[window]).astype(jnp.int32)
        segment = lax.dynamic_slice(record, (jnp.int32(0), window_start), (channels, seg_len))
        whitened = whiten(segment)
        source_rows = jnp.take(whitened, source_channel, axis=0).astype(jnp.float32)
        source_part = source_rows[:, L // 2:L // 2 + WL]
        padded = jnp.concatenate([source_part, jnp.zeros((source_part.shape[0], L), jnp.float32)], axis=1)
        source_spec = jnp.fft.rfft(padded, axis=-1)
        recv_spec = jnp.fft.rfft(whitened.astype(jnp.float32), axis=-1)

        def per_source(spec_row):
            full = jnp.fft.irfft(jnp.conj(spec_row)[None, :] * recv_spec, n=seg_len, axis=-1)
            return full[:, :L].astype(jnp.float32)
        lagged = lax.map(per_source, source_spec)
        return (running + lagged, None)
    initial = jnp.zeros((source_channel.shape[0], channels, L), jnp.float32)
    lagged, _ = lax.scan(one_window, initial, jnp.arange(N_SRC, dtype=jnp.int32))
    factor = 1.0 / float(WL * N_SRC) ** 0.5
    in_band = (channel_ids[None, :] >= band_edges[:, 0:1]) & (channel_ids[None, :] < band_edges[:, 1:2])
    in_band = in_band & (channel_ids[None, :] != source_channel[:, None])
    return jnp.where(in_band[:, :, None], lagged * factor, jnp.float32(0.0))
```

```python
import jax
import jax.numpy as jnp
from jax import lax
from jax.experimental import pallas as pl
from jax.experimental.pallas import tpu as pltpu
from jax.sharding import PartitionSpec as P

WL = 2560
L = 256
SEG = WL + L
LANES = 128
TILES = SEG // LANES
BODY = WL // LANES
SLOT = 24
STEP = 16
EPSILON = 1e-06

VMEM = pl.BlockSpec(memory_space=pltpu.VMEM)
SMEM = pl.BlockSpec(memory_space=pltpu.SMEM)


def lane_index(rows):
    return lax.broadcasted_iota(jnp.int32, (rows, LANES), 1)


def prepare_kernel(where_ref, row_ref, record_ref, white_ref, slots_ref, line_ref):
    chan_dev = record_ref.shape[0]
    start = where_ref[0]
    first = start // LANES
    rest = start - first * LANES
    last = record_ref.shape[1] // LANES - 1
    lane = lane_index(chan_dev)
    shift = lax.rem(LANES - rest, LANES)

    def rolled(tile):
        at = pl.multiple_of(jnp.minimum(first + tile, last) * LANES, LANES)
        return pltpu.roll(record_ref[:, pl.ds(at, LANES)].astype(jnp.float32), shift, 1)

    segment = []
    total = jnp.zeros((chan_dev, LANES), jnp.float32)
    left = rolled(0)
    for tile in range(TILES):
        right = rolled(tile + 1)
        piece = jnp.where(lane < LANES - rest, left, right)
        segment.append(piece)
        total = total + piece * piece
        left = right
    power = jnp.sum(total, axis=1, keepdims=True) / SEG
    spread = jnp.broadcast_to(jnp.sqrt(power + EPSILON), (chan_dev, LANES))
    line_ref[...] = jnp.zeros_like(line_ref)
    for tile in range(TILES):
        white = (segment[tile] / spread).astype(jnp.bfloat16)
        white_ref[:, tile * LANES : (tile + 1) * LANES] = white
        if 1 <= tile <= BODY:
            line_ref[pl.ds(tile - 1, chan_dev, stride=SLOT), :] = white.astype(jnp.float32)
    for slot in range(slots_ref.shape[0]):
        at = pl.multiple_of(row_ref[slot] * SLOT, 8)
        slots_ref[slot] = line_ref[pl.ds(at, SLOT), :].astype(jnp.bfloat16)


def spread_kernel(owner_ref, slots_ref, out_ref):
    row = slots_ref[owner_ref[0]]
    for slot in range(out_ref.shape[0]):
        out_ref[slot] = row


def correlate_kernel(source_ref, white_ref, out_ref, line_ref, a_ref, b_ref, part_ref):
    count = source_ref.shape[0]
    chan_dev = white_ref.shape[0]
    lane = lane_index(count)
    for slot in range(count):
        line_ref[slot * SLOT : (slot + 1) * SLOT, :] = source_ref[slot].astype(jnp.float32)
    coarse = LANES // STEP
    pieces = [line_ref[pl.ds(tile, count, stride=SLOT), :] for tile in range(BODY)]
    zero = jnp.zeros((count, LANES), jnp.float32)
    for m in range(coarse):
        shift = STEP * m
        left = zero
        for tile in range(BODY + 1):
            right = pieces[tile] if tile < BODY else zero
            if m:
                right = pltpu.roll(right, shift, 1) if tile < BODY else zero
                value = jnp.where(lane < shift, left, right)
            else:
                value = right
            a_ref[m * count : (m + 1) * count, tile * LANES : (tile + 1) * LANES] = value.astype(jnp.bfloat16)
            left = right
    lane = lane_index(chan_dev)
    pieces = [white_ref[:, tile * LANES : (tile + 1) * LANES].astype(jnp.float32) for tile in range(TILES)]
    for l in range(STEP):
        left = pltpu.roll(pieces[0], LANES - l, 1) if l else pieces[0]
        for tile in range(TILES):
            right = pieces[(tile + 1) % TILES]
            if l:
                right = pltpu.roll(right, LANES - l, 1)
                value = jnp.where(lane < LANES - l, left, right)
            else:
                value = left
            b_ref[l * chan_dev : (l + 1) * chan_dev, tile * LANES : (tile + 1) * LANES] = value.astype(jnp.bfloat16)
            left = right
    depth = (BODY + 1) * LANES
    half = count // 2
    for high in range(L // LANES):
        product = lax.dot_general(
            a_ref[...],
            b_ref[:, high * LANES : high * LANES + depth],
            (((1,), (1,)), ((), ())),
            preferred_element_type=jnp.float32,
        )
        for low in range(coarse):
            m = high * coarse + low
            for j in range(2):
                row = low * count + j * half
                for n in range(STEP * chan_dev // LANES):
                    part_ref[n, pl.ds(j * STEP + m, half, stride=2 * STEP), :] = product[
                        row : row + half, n * LANES : (n + 1) * LANES
                    ]
    for n in range(STEP * chan_dev // LANES):
        out_ref[:, n * LANES : (n + 1) * LANES] = part_ref[n].astype(jnp.bfloat16)


def local(record, source_channel, band_edges, offsets):
    chan_dev = record.shape[0]
    recv_index = lax.axis_index("recv")
    src_index = lax.axis_index("src")
    src_count = lax.axis_size("src")
    source_total = source_channel.shape[0]
    per = source_total // src_count
    slot_channel = source_channel.reshape(src_count, per).T.reshape(source_total)
    window_start = lax.dynamic_slice(offsets, (src_index,), (1,))
    rows = jnp.clip(slot_channel - recv_index * chan_dev, 0, chan_dev - 1)
    owner = lax.dynamic_slice(slot_channel, (recv_index,), (1,)) // chan_dev
    params = pltpu.CompilerParams(vmem_limit_bytes=40 * 1024 * 1024)
    slots = jax.ShapeDtypeStruct((source_total, SLOT, LANES), jnp.bfloat16)
    white, out_rows = pl.pallas_call(
        prepare_kernel,
        out_shape=(jax.ShapeDtypeStruct((chan_dev, SEG), jnp.bfloat16), slots),
        in_specs=[SMEM, SMEM, VMEM],
        out_specs=(VMEM, VMEM),
        scratch_shapes=[pltpu.VMEM((chan_dev * SLOT, LANES), jnp.float32)],
        compiler_params=params,
        name="prepare",
    )(window_start, rows, record)
    in_rows = lax.all_to_all(out_rows, "recv", split_axis=0, concat_axis=0, tiled=True)
    own_row = pl.pallas_call(
        spread_kernel,
        out_shape=slots,
        in_specs=[SMEM, VMEM],
        out_specs=VMEM,
        compiler_params=params,
        name="spread",
    )(owner, in_rows)
    sources = lax.all_to_all(own_row, "recv", split_axis=0, concat_axis=0, tiled=True)
    wide = STEP * chan_dev
    partial = pl.pallas_call(
        correlate_kernel,
        out_shape=jax.ShapeDtypeStruct((source_total * (L // STEP), wide), jnp.bfloat16),
        in_specs=[VMEM, VMEM],
        out_specs=VMEM,
        scratch_shapes=[
            pltpu.VMEM((source_total * SLOT, LANES), jnp.float32),
            pltpu.VMEM((source_total * LANES // STEP, (BODY + 1) * LANES), jnp.bfloat16),
            pltpu.VMEM((wide, SEG), jnp.bfloat16),
            pltpu.VMEM((wide // LANES, source_total * (L // STEP), LANES), jnp.float32),
        ],
        compiler_params=params,
        name="correlate",
    )(sources, white)
    partial = partial.reshape(src_count, per * (L // STEP), wide)
    windows = lax.all_to_all(partial, "src", split_axis=0, concat_axis=0, tiled=True)
    stacked = jnp.sum(windows.astype(jnp.float32), axis=0)
    stacked = stacked.reshape(per, L // STEP, STEP, chan_dev).transpose(0, 3, 1, 2).reshape(per, chan_dev, L)
    factor = 1.0 / float(WL * src_count) ** 0.5
    own_channel = lax.dynamic_slice_in_dim(source_channel, src_index * per, per, 0)
    own_edges = lax.dynamic_slice_in_dim(band_edges, src_index * per, per, 0)
    channel_ids = recv_index * chan_dev + jnp.arange(chan_dev, dtype=jnp.int32)
    in_band = (channel_ids[None, :] >= own_edges[:, 0:1]) & (channel_ids[None, :] < own_edges[:, 1:2])
    in_band = in_band & (channel_ids[None, :] != own_channel[:, None])
    return jnp.where(in_band[:, :, None], stacked * factor, jnp.float32(0.0))


def solution(mesh):
    in_specs = (P("recv", "src"), P(), P(), P())
    out_specs = P("src", "recv", None)
    return jax.shard_map(local, mesh=mesh, in_specs=in_specs, out_specs=out_specs, check_vma=False)
```

```python
import functools

import jax
import jax.numpy as jnp
from jax import lax
from jax.experimental import pallas as pl
from jax.experimental.pallas import tpu as pltpu
from jax.sharding import PartitionSpec as P

WL = 2560
L = 256
SEG = WL + L
LANES = 128
TILES = SEG // LANES
BODY = WL // LANES
STEP = 16
COARSE = LANES // STEP
DEPTH = WL + LANES
EPSILON = 1e-06
CORES = 2
PLANS = ((4, 2), (6, 4), (16, 1))

VMEM = pl.BlockSpec(memory_space=pltpu.VMEM)
SMEM = pl.BlockSpec(memory_space=pltpu.SMEM)
PARAMS = pltpu.CompilerParams(vmem_limit_bytes=40 * 1024 * 1024)


def iota(shape, dim):
    return lax.broadcasted_iota(jnp.int32, shape, dim)


def column(row):
    count = row.shape[1]
    square = iota((count, count), 0) == iota((count, count), 1)
    return jnp.sum(jnp.where(square, jnp.broadcast_to(row, (count, count)), 0), axis=1, keepdims=True)


def one_hot(mask):
    return jnp.where(mask, 1.0, 0.0).astype(jnp.bfloat16)


def prepare_kernel(plan, offsets_ref, channel_ref, record_ref, white_ref, send_ref):
    slots, split = plan
    chan_dev = record_ref.shape[0]
    start = offsets_ref[lax.axis_index("src")]
    first = start // LANES
    rest = start - first * LANES
    last = record_ref.shape[1] // LANES - 1
    lane = iota((chan_dev, LANES), 1)
    shift = lax.rem(LANES - rest, LANES)

    def rolled(tile):
        at = pl.multiple_of(jnp.minimum(first + tile, last) * LANES, LANES)
        return pltpu.roll(record_ref[:, pl.ds(at, LANES)].astype(jnp.float32), shift, 1)

    segment = []
    total = jnp.zeros((chan_dev, LANES), jnp.float32)
    left = rolled(0)
    for tile in range(TILES):
        right = rolled(tile + 1)
        piece = jnp.where(lane < LANES - rest, left, right)
        segment.append(piece)
        total = total + piece * piece
        left = right
    power = jnp.sum(total, axis=1, keepdims=True) / SEG
    spread = jnp.broadcast_to(jnp.sqrt(power + EPSILON), (chan_dev, LANES))
    for tile in range(TILES):
        white_ref[:, tile * LANES : (tile + 1) * LANES] = (segment[tile] / spread).astype(jnp.bfloat16)
    base = lax.axis_index("recv") * chan_dev
    source = column(channel_ref[...])
    count = source.shape[0]
    mine = iota((count, chan_dev), 1) + base
    is_source = jnp.sum(jnp.where(source == mine, 1, 0), axis=0, keepdims=True)
    before = jnp.sum(jnp.where((source >= base) & (source < mine), 1, 0), axis=0, keepdims=True)
    row = iota((slots * split, chan_dev), 0)
    width = WL // split
    packed = None
    for part in range(split):
        pick = (before == row - part * slots) & (is_source > 0) & (row >= part * slots) & (row < (part + 1) * slots)
        term = jnp.dot(
            one_hot(pick),
            white_ref[:, L // 2 + part * width : L // 2 + (part + 1) * width],
            preferred_element_type=jnp.float32,
        )
        packed = term if packed is None else packed + term
    packed = packed.astype(jnp.bfloat16)
    for dest in range(send_ref.shape[0]):
        send_ref[dest] = packed


def shift_kernel(white_ref, shifted_ref, rows_ref):
    chan_dev = white_ref.shape[0]
    white = white_ref[...]
    for l in range(STEP):
        rows_ref[l * chan_dev : (l + 1) * chan_dev, :] = pltpu.roll(white, SEG - l, 1) if l else white
    for tile in range(TILES):
        at = slice(tile * LANES, (tile + 1) * LANES)
        shifted_ref[at, :] = rows_ref[:, at].T


def correlate_kernel(plan, channel_ref, near_ref, far_ref, shifted_ref, out_ref, a_ref, part_ref):
    slots, split = plan
    wide = shifted_ref.shape[1]
    chan_dev = wide // STEP
    count = channel_ref.shape[1]
    half = count // 2
    core = lax.rem(lax.axis_index("recv"), CORES)
    order = iota((count, count), 0)
    order = jnp.where(order < half, 2 * order, 2 * (order - half) + 1)
    every = jnp.broadcast_to(channel_ref[...], (count, count))
    source = jnp.sum(jnp.where(order == iota((count, count), 1), every, 0), axis=1, keepdims=True)
    owner = source // chan_dev
    place = jnp.sum(jnp.where((every >= owner * chan_dev) & (every < source), 1, 0), axis=1, keepdims=True)
    at = (owner // CORES) * (slots * split) + place
    is_near = lax.rem(owner, CORES) == core
    groups = near_ref.shape[0]
    total = groups * slots * split
    width = WL // split
    near = near_ref[...].reshape(total, width)
    far = far_ref[...].reshape(total, width)
    pieces = []
    for part in range(split):
        hit = iota((count, total), 1) == at + part * slots
        gathered = jnp.dot(one_hot(hit & is_near), near, preferred_element_type=jnp.float32)
        gathered = gathered + jnp.dot(one_hot(hit & ~is_near), far, preferred_element_type=jnp.float32)
        pieces.append(gathered.astype(jnp.bfloat16))
    rows = jnp.concatenate(pieces + [jnp.zeros((count, LANES), jnp.bfloat16)], axis=1)
    for m in range(COARSE):
        a_ref[m * count : (m + 1) * count, :] = pltpu.roll(rows, STEP * m, 1) if m else rows
    for high in range(L // LANES):
        product = jnp.dot(
            a_ref[...],
            shifted_ref[high * LANES : high * LANES + DEPTH, :],
            preferred_element_type=jnp.float32,
        )
        for low in range(COARSE):
            m = high * COARSE + low
            for j in range(2):
                row = low * count + j * half
                for n in range(wide // LANES):
                    part_ref[n, pl.ds(j * STEP + m, half, stride=2 * STEP), :] = product[
                        row : row + half, n * LANES : (n + 1) * LANES
                    ]
    for n in range(wide // LANES):
        out_ref[:, n * LANES : (n + 1) * LANES] = part_ref[n].astype(jnp.bfloat16)


def stack(plan, record, source_channel, band_edges, offsets):
    slots, split = plan
    chan_dev = record.shape[0]
    recv_index = lax.axis_index("recv")
    src_index = lax.axis_index("src")
    recv_count = lax.axis_size("recv")
    src_count = lax.axis_size("src")
    source_total = source_channel.shape[0]
    per = source_total // src_count
    wide = STEP * chan_dev
    groups = recv_count // CORES
    channel_row = source_channel.reshape(1, source_total)
    white, send = pl.pallas_call(
        functools.partial(prepare_kernel, plan),
        out_shape=(
            jax.ShapeDtypeStruct((chan_dev, SEG), jnp.bfloat16),
            jax.ShapeDtypeStruct((groups, slots * split, WL // split), jnp.bfloat16),
        ),
        in_specs=[SMEM, VMEM, VMEM],
        out_specs=(VMEM, VMEM),
        compiler_params=PARAMS,
        name="prepare",
    )(offsets, channel_row, record)
    near = lax.all_to_all(
        send,
        "recv",
        split_axis=0,
        concat_axis=0,
        tiled=True,
        axis_index_groups=[list(range(core, recv_count, CORES)) for core in range(CORES)],
    )
    far = lax.ppermute(near, "recv", [(i, i ^ 1) for i in range(recv_count)])
    shifted = pl.pallas_call(
        shift_kernel,
        out_shape=jax.ShapeDtypeStruct((SEG, wide), jnp.bfloat16),
        in_specs=[VMEM],
        out_specs=VMEM,
        scratch_shapes=[pltpu.VMEM((wide, SEG), jnp.bfloat16)],
        compiler_params=PARAMS,
        cost_estimate=pl.CostEstimate(flops=10**9, bytes_accessed=4 * 10**6, transcendentals=0),
        name="shift",
    )(white)
    partial = pl.pallas_call(
        functools.partial(correlate_kernel, plan),
        out_shape=jax.ShapeDtypeStruct((source_total * (L // STEP), wide), jnp.bfloat16),
        in_specs=[VMEM, VMEM, VMEM, VMEM],
        out_specs=VMEM,
        scratch_shapes=[
            pltpu.VMEM((source_total * COARSE, DEPTH), jnp.bfloat16),
            pltpu.VMEM((wide // LANES, source_total * (L // STEP), LANES), jnp.float32),
        ],
        compiler_params=PARAMS,
        name="correlate",
    )(channel_row, near, far, shifted)
    partial = partial.reshape(src_count, per * (L // STEP), wide)
    windows = lax.all_to_all(partial, "src", split_axis=0, concat_axis=0, tiled=True)
    stacked = jnp.sum(windows.astype(jnp.float32), axis=0)
    stacked = stacked.reshape(per, L // STEP, STEP, chan_dev).transpose(0, 3, 1, 2).reshape(per, chan_dev, L)
    factor = 1.0 / float(WL * src_count) ** 0.5
    own_channel = lax.dynamic_slice_in_dim(source_channel, src_index * per, per, 0)
    own_edges = lax.dynamic_slice_in_dim(band_edges, src_index * per, per, 0)
    channel_ids = recv_index * chan_dev + jnp.arange(chan_dev, dtype=jnp.int32)
    in_band = (channel_ids[None, :] >= own_edges[:, 0:1]) & (channel_ids[None, :] < own_edges[:, 1:2])
    in_band = in_band & (channel_ids[None, :] != own_channel[:, None])
    return jnp.where(in_band[:, :, None], stacked * factor, jnp.float32(0.0))


def local(record, source_channel, band_edges, offsets):
    recv_count = lax.axis_size("recv")
    owners = source_channel // record.shape[0]
    blocks = jnp.arange(recv_count, dtype=jnp.int32)
    most = jnp.max(jnp.sum((owners[None, :] == blocks[:, None]).astype(jnp.int32), axis=1))
    choice = sum((most > slots).astype(jnp.int32) for slots, _ in PLANS[:-1])
    return lax.switch(
        choice,
        [functools.partial(stack, plan) for plan in PLANS],
        record,
        source_channel,
        band_edges,
        offsets,
    )


def solution(mesh):
    in_specs = (P("recv", "src"), P(), P(), P())
    out_specs = P("src", "recv", None)
    return jax.shard_map(local, mesh=mesh, in_specs=in_specs, out_specs=out_specs, check_vma=False)
```

```python
import functools

import jax
import jax.numpy as jnp
from jax import lax
from jax.experimental import pallas as pl
from jax.experimental.pallas import tpu as pltpu
from jax.sharding import PartitionSpec as P

WL = 2560
L = 256
SEG = WL + L
LANES = 128
TILES = SEG // LANES
BODY = WL // LANES
STEP = 16
COARSE = LANES // STEP
DEPTH = WL + LANES
EPSILON = 1e-06
CORES = 2
PLANS = ((3, 5, 16), (4, 2, 8), (6, 4, 24), (16, 1, 16))

VMEM = pl.BlockSpec(memory_space=pltpu.VMEM)
SMEM = pl.BlockSpec(memory_space=pltpu.SMEM)
PARAMS = pltpu.CompilerParams(vmem_limit_bytes=40 * 1024 * 1024)


def iota(shape, dim):
    return lax.broadcasted_iota(jnp.int32, shape, dim)


def column(row):
    count = row.shape[1]
    square = iota((count, count), 0) == iota((count, count), 1)
    return jnp.sum(jnp.where(square, jnp.broadcast_to(row, (count, count)), 0), axis=1, keepdims=True)


def one_hot(mask):
    return jnp.where(mask, 1.0, 0.0).astype(jnp.bfloat16)


def prepare_kernel(plan, offsets_ref, channel_ref, record_ref, white_ref, send_ref):
    slots, split, rows = plan
    chan_dev = record_ref.shape[0]
    start = offsets_ref[lax.axis_index("src")]
    first = start // LANES
    rest = start - first * LANES
    last = record_ref.shape[1] // LANES - 1
    lane = iota((chan_dev, LANES), 1)
    shift = lax.rem(LANES - rest, LANES)

    def rolled(tile):
        at = pl.multiple_of(jnp.minimum(first + tile, last) * LANES, LANES)
        return pltpu.roll(record_ref[:, pl.ds(at, LANES)].astype(jnp.float32), shift, 1)

    segment = []
    total = jnp.zeros((chan_dev, LANES), jnp.float32)
    left = rolled(0)
    for tile in range(TILES):
        right = rolled(tile + 1)
        piece = jnp.where(lane < LANES - rest, left, right)
        segment.append(piece)
        total = total + piece * piece
        left = right
    power = jnp.sum(total, axis=1, keepdims=True) / SEG
    spread = jnp.broadcast_to(jnp.sqrt(power + EPSILON), (chan_dev, LANES))
    for tile in range(TILES):
        white_ref[:, tile * LANES : (tile + 1) * LANES] = (segment[tile] / spread).astype(jnp.bfloat16)
    base = lax.axis_index("recv") * chan_dev
    source = column(channel_ref[...])
    mine = iota((source.shape[0], chan_dev), 1) + base
    is_source = jnp.sum(jnp.where(source == mine, 1, 0), axis=0, keepdims=True)
    before = jnp.sum(jnp.where((source >= base) & (source < mine), 1, 0), axis=0, keepdims=True)
    row = iota((rows, chan_dev), 0)
    width = WL // split
    packed = None
    for part in range(split):
        pick = (before == row - part * slots) & (is_source > 0) & (row >= part * slots) & (row < (part + 1) * slots)
        term = jnp.dot(
            one_hot(pick),
            white_ref[:, L // 2 + part * width : L // 2 + (part + 1) * width],
            preferred_element_type=jnp.float32,
        )
        packed = term if packed is None else packed + term
    packed = packed.astype(jnp.bfloat16)
    for dest in range(send_ref.shape[0]):
        send_ref[dest] = packed


def shift_kernel(white_ref, shifted_ref, rows_ref):
    chan_dev = white_ref.shape[0]
    white = white_ref[...]
    for l in range(STEP):
        rows_ref[l * chan_dev : (l + 1) * chan_dev, :] = pltpu.roll(white, SEG - l, 1) if l else white
    for tile in range(TILES):
        at = slice(tile * LANES, (tile + 1) * LANES)
        shifted_ref[at, :] = rows_ref[:, at].T


def correlate_kernel(plan, channel_ref, near_ref, far_ref, shifted_ref, out_ref, a_ref, part_ref):
    slots, split, rows = plan
    wide = shifted_ref.shape[1]
    chan_dev = wide // STEP
    count = channel_ref.shape[1]
    half = count // 2
    core = lax.rem(lax.axis_index("recv"), CORES)
    order = iota((count, count), 0)
    order = jnp.where(order < half, 2 * order, 2 * (order - half) + 1)
    every = jnp.broadcast_to(channel_ref[...], (count, count))
    source = jnp.sum(jnp.where(order == iota((count, count), 1), every, 0), axis=1, keepdims=True)
    owner = source // chan_dev
    place = jnp.sum(jnp.where((every >= owner * chan_dev) & (every < source), 1, 0), axis=1, keepdims=True)
    at = (owner // CORES) * rows + place
    is_near = lax.rem(owner, CORES) == core
    groups = near_ref.shape[0]
    total = groups * rows
    width = WL // split
    near = near_ref[...].reshape(total, width)
    far = far_ref[...].reshape(total, width)
    pieces = []
    for part in range(split):
        hit = iota((count, total), 1) == at + part * slots
        gathered = jnp.dot(one_hot(hit & is_near), near, preferred_element_type=jnp.float32)
        gathered = gathered + jnp.dot(one_hot(hit & ~is_near), far, preferred_element_type=jnp.float32)
        pieces.append(gathered.astype(jnp.bfloat16))
    joined = jnp.concatenate(pieces + [jnp.zeros((count, LANES), jnp.bfloat16)], axis=1)
    for m in range(COARSE):
        a_ref[m * count : (m + 1) * count, :] = pltpu.roll(joined, STEP * m, 1) if m else joined
    for high in range(L // LANES):
        product = jnp.dot(
            a_ref[...],
            shifted_ref[high * LANES : high * LANES + DEPTH, :],
            preferred_element_type=jnp.float32,
        )
        for low in range(COARSE):
            m = high * COARSE + low
            for j in range(2):
                row = low * count + j * half
                for n in range(wide // LANES):
                    part_ref[n, pl.ds(j * STEP + m, half, stride=2 * STEP), :] = product[
                        row : row + half, n * LANES : (n + 1) * LANES
                    ]
    for n in range(wide // LANES):
        out_ref[:, n * LANES : (n + 1) * LANES] = part_ref[n].astype(jnp.bfloat16)


def stack(plan, record, source_channel, band_edges, offsets):
    slots, split, rows = plan
    chan_dev = record.shape[0]
    recv_index = lax.axis_index("recv")
    src_index = lax.axis_index("src")
    recv_count = lax.axis_size("recv")
    src_count = lax.axis_size("src")
    source_total = source_channel.shape[0]
    per = source_total // src_count
    wide = STEP * chan_dev
    groups = recv_count // CORES
    channel_row = source_channel.reshape(1, source_total)
    white, send = pl.pallas_call(
        functools.partial(prepare_kernel, plan),
        out_shape=(
            jax.ShapeDtypeStruct((chan_dev, SEG), jnp.bfloat16),
            jax.ShapeDtypeStruct((groups, rows, WL // split), jnp.bfloat16),
        ),
        in_specs=[SMEM, VMEM, VMEM],
        out_specs=(VMEM, VMEM),
        compiler_params=PARAMS,
        name="prepare",
    )(offsets, channel_row, record)
    near = lax.all_to_all(
        send,
        "recv",
        split_axis=0,
        concat_axis=0,
        tiled=True,
        axis_index_groups=[list(range(core, recv_count, CORES)) for core in range(CORES)],
    )
    far = lax.ppermute(near, "recv", [(i, i ^ 1) for i in range(recv_count)])
    shifted = pl.pallas_call(
        shift_kernel,
        out_shape=jax.ShapeDtypeStruct((SEG, wide), jnp.bfloat16),
        in_specs=[VMEM],
        out_specs=VMEM,
        scratch_shapes=[pltpu.VMEM((wide, SEG), jnp.bfloat16)],
        compiler_params=PARAMS,
        cost_estimate=pl.CostEstimate(flops=10**9, bytes_accessed=4 * 10**6, transcendentals=0),
        name="shift",
    )(white)
    partial = pl.pallas_call(
        functools.partial(correlate_kernel, plan),
        out_shape=jax.ShapeDtypeStruct((source_total * (L // STEP), wide), jnp.bfloat16),
        in_specs=[VMEM, VMEM, VMEM, VMEM],
        out_specs=VMEM,
        scratch_shapes=[
            pltpu.VMEM((source_total * COARSE, DEPTH), jnp.bfloat16),
            pltpu.VMEM((wide // LANES, source_total * (L // STEP), LANES), jnp.float32),
        ],
        compiler_params=PARAMS,
        name="correlate",
    )(channel_row, near, far, shifted)
    partial = partial.reshape(src_count, per * (L // STEP), wide)
    windows = lax.all_to_all(partial, "src", split_axis=0, concat_axis=0, tiled=True)
    stacked = jnp.sum(windows.astype(jnp.float32), axis=0)
    stacked = stacked.reshape(per, L // STEP, STEP, chan_dev).transpose(0, 3, 1, 2).reshape(per, chan_dev, L)
    factor = 1.0 / float(WL * src_count) ** 0.5
    own_channel = lax.dynamic_slice_in_dim(source_channel, src_index * per, per, 0)
    own_edges = lax.dynamic_slice_in_dim(band_edges, src_index * per, per, 0)
    channel_ids = recv_index * chan_dev + jnp.arange(chan_dev, dtype=jnp.int32)
    in_band = (channel_ids[None, :] >= own_edges[:, 0:1]) & (channel_ids[None, :] < own_edges[:, 1:2])
    in_band = in_band & (channel_ids[None, :] != own_channel[:, None])
    return jnp.where(in_band[:, :, None], stacked * factor, jnp.float32(0.0))


def local(record, source_channel, band_edges, offsets):
    blocks = jnp.arange(lax.axis_size("recv"), dtype=jnp.int32)
    owners = source_channel // record.shape[0]
    held = jnp.sum((owners[None, :] == blocks[:, None]).astype(jnp.int32), axis=1)
    choice = jnp.max(sum((held > plan[0]).astype(jnp.int32) for plan in PLANS[:-1]))
    return lax.switch(
        choice,
        [functools.partial(stack, plan) for plan in PLANS],
        record,
        source_channel,
        band_edges,
        offsets,
    )


def solution(mesh):
    in_specs = (P("recv", "src"), P(), P(), P())
    out_specs = P("src", "recv", None)
    return jax.shard_map(local, mesh=mesh, in_specs=in_specs, out_specs=out_specs, check_vma=False)
```

```python
import functools

import jax
import jax.numpy as jnp
from jax import lax
from jax.experimental import pallas as pl
from jax.experimental.pallas import tpu as pltpu
from jax.sharding import PartitionSpec as P

WL = 2560
L = 256
SEG = WL + L
LANES = 128
TILES = SEG // LANES
BODY = WL // LANES
STEP = 16
COARSE = LANES // STEP
DEPTH = WL + LANES
EPSILON = 1e-06
CORES = 2
PLANS = ((3, 5, 16), (4, 2, 8), (6, 4, 24), (16, 1, 16))

VMEM = pl.BlockSpec(memory_space=pltpu.VMEM)
SMEM = pl.BlockSpec(memory_space=pltpu.SMEM)
PARAMS = pltpu.CompilerParams(vmem_limit_bytes=40 * 1024 * 1024)


def iota(shape, dim):
    return lax.broadcasted_iota(jnp.int32, shape, dim)


def column(row):
    count = row.shape[1]
    square = iota((count, count), 0) == iota((count, count), 1)
    return jnp.sum(jnp.where(square, jnp.broadcast_to(row, (count, count)), 0), axis=1, keepdims=True)


def one_hot(mask):
    return jnp.where(mask, 1.0, 0.0).astype(jnp.bfloat16)


def prepare_kernel(plan, offsets_ref, channel_ref, record_ref, white_ref, send_ref):
    slots, split, rows = plan
    chan_dev = record_ref.shape[0]
    start = offsets_ref[lax.axis_index("src")]
    first = start // LANES
    rest = start - first * LANES
    last = record_ref.shape[1] // LANES - 1
    lane = iota((chan_dev, LANES), 1)
    shift = lax.rem(LANES - rest, LANES)

    def rolled(tile):
        at = pl.multiple_of(jnp.minimum(first + tile, last) * LANES, LANES)
        return pltpu.roll(record_ref[:, pl.ds(at, LANES)].astype(jnp.float32), shift, 1)

    segment = []
    total = jnp.zeros((chan_dev, LANES), jnp.float32)
    left = rolled(0)
    for tile in range(TILES):
        right = rolled(tile + 1)
        piece = jnp.where(lane < LANES - rest, left, right)
        segment.append(piece)
        total = total + piece * piece
        left = right
    power = jnp.sum(total, axis=1, keepdims=True) / SEG
    spread = jnp.broadcast_to(jnp.sqrt(power + EPSILON), (chan_dev, LANES))
    for tile in range(TILES):
        white_ref[:, tile * LANES : (tile + 1) * LANES] = (segment[tile] / spread).astype(jnp.bfloat16)
    base = lax.axis_index("recv") * chan_dev
    source = column(channel_ref[...])
    mine = iota((source.shape[0], chan_dev), 1) + base
    is_source = jnp.sum(jnp.where(source == mine, 1, 0), axis=0, keepdims=True)
    before = jnp.sum(jnp.where((source >= base) & (source < mine), 1, 0), axis=0, keepdims=True)
    row = iota((rows, chan_dev), 0)
    width = WL // split
    packed = None
    for part in range(split):
        pick = (before == row - part * slots) & (is_source > 0) & (row >= part * slots) & (row < (part + 1) * slots)
        term = jnp.dot(
            one_hot(pick),
            white_ref[:, L // 2 + part * width : L // 2 + (part + 1) * width],
            preferred_element_type=jnp.float32,
        )
        packed = term if packed is None else packed + term
    packed = packed.astype(jnp.bfloat16)
    for dest in range(send_ref.shape[0]):
        send_ref[dest] = packed


def shift_kernel(white_ref, shifted_ref, rows_ref):
    chan_dev = white_ref.shape[0]
    white = white_ref[...]
    for l in range(STEP):
        rows_ref[l * chan_dev : (l + 1) * chan_dev, :] = pltpu.roll(white, SEG - l, 1) if l else white
    for tile in range(TILES):
        at = slice(tile * LANES, (tile + 1) * LANES)
        shifted_ref[at, :] = rows_ref[:, at].T


def correlate_kernel(plan, channel_ref, near_ref, far_ref, shifted_ref, out_ref, a_ref, part_ref):
    slots, split, rows = plan
    wide = shifted_ref.shape[1]
    chan_dev = wide // STEP
    count = channel_ref.shape[1]
    half = count // 2
    core = lax.rem(lax.axis_index("recv"), CORES)
    order = iota((count, count), 0)
    order = jnp.where(order < half, 2 * order, 2 * (order - half) + 1)
    every = jnp.broadcast_to(channel_ref[...], (count, count))
    source = jnp.sum(jnp.where(order == iota((count, count), 1), every, 0), axis=1, keepdims=True)
    owner = source // chan_dev
    place = jnp.sum(jnp.where((every >= owner * chan_dev) & (every < source), 1, 0), axis=1, keepdims=True)
    at = (owner // CORES) * rows + place
    groups = near_ref.shape[0]
    total = groups * rows
    width = WL // split
    both = jnp.concatenate([near_ref[...].reshape(total, width), far_ref[...].reshape(total, width)], axis=0)
    at = jnp.where(lax.rem(owner, CORES) == core, at, at + total)
    hits = [one_hot(iota((count, CORES * total), 1) == at + part * slots) for part in range(split)]
    gathered = jnp.dot(jnp.concatenate(hits, axis=0), both, preferred_element_type=jnp.float32).astype(jnp.bfloat16)
    pieces = [gathered[part * count : (part + 1) * count] for part in range(split)]
    joined = jnp.concatenate(pieces + [jnp.zeros((count, LANES), jnp.bfloat16)], axis=1)
    for m in range(COARSE):
        a_ref[m * count : (m + 1) * count, :] = pltpu.roll(joined, STEP * m, 1) if m else joined
    for high in range(L // LANES):
        product = jnp.dot(
            a_ref[...],
            shifted_ref[high * LANES : high * LANES + DEPTH, :],
            preferred_element_type=jnp.float32,
        )
        for low in range(COARSE):
            m = high * COARSE + low
            for j in range(2):
                row = low * count + j * half
                for n in range(wide // LANES):
                    part_ref[n, pl.ds(j * STEP + m, half, stride=2 * STEP), :] = product[
                        row : row + half, n * LANES : (n + 1) * LANES
                    ]
    for n in range(wide // LANES):
        out_ref[:, n * LANES : (n + 1) * LANES] = part_ref[n].astype(jnp.bfloat16)


def stack(plan, record, source_channel, band_edges, offsets):
    slots, split, rows = plan
    chan_dev = record.shape[0]
    recv_index = lax.axis_index("recv")
    src_index = lax.axis_index("src")
    recv_count = lax.axis_size("recv")
    src_count = lax.axis_size("src")
    source_total = source_channel.shape[0]
    per = source_total // src_count
    wide = STEP * chan_dev
    channel_row = source_channel.reshape(1, source_total)
    white, send = pl.pallas_call(
        functools.partial(prepare_kernel, plan),
        out_shape=(
            jax.ShapeDtypeStruct((chan_dev, SEG), jnp.bfloat16),
            jax.ShapeDtypeStruct((recv_count // CORES, rows, WL // split), jnp.bfloat16),
        ),
        in_specs=[SMEM, VMEM, VMEM],
        out_specs=(VMEM, VMEM),
        compiler_params=PARAMS,
        name="prepare",
    )(offsets, channel_row, record)
    near = lax.all_to_all(
        send,
        "recv",
        split_axis=0,
        concat_axis=0,
        tiled=True,
        axis_index_groups=[list(range(core, recv_count, CORES)) for core in range(CORES)],
    )
    far = lax.ppermute(near, "recv", [(i, i ^ 1) for i in range(recv_count)])
    far, source_channel, band_edges = lax.optimization_barrier((far, source_channel, band_edges))
    own_channel = lax.dynamic_slice_in_dim(source_channel, src_index * per, per, 0)
    own_edges = lax.dynamic_slice_in_dim(band_edges, src_index * per, per, 0)
    channel_ids = recv_index * chan_dev + jnp.arange(chan_dev, dtype=jnp.int32)
    keep = (channel_ids[None, :] >= own_edges[:, 0:1]) & (channel_ids[None, :] < own_edges[:, 1:2])
    keep = keep & (channel_ids[None, :] != own_channel[:, None])
    shifted = pl.pallas_call(
        shift_kernel,
        out_shape=jax.ShapeDtypeStruct((SEG, wide), jnp.bfloat16),
        in_specs=[VMEM],
        out_specs=VMEM,
        scratch_shapes=[pltpu.VMEM((wide, SEG), jnp.bfloat16)],
        compiler_params=PARAMS,
        cost_estimate=pl.CostEstimate(flops=10**9, bytes_accessed=4 * 10**6, transcendentals=0),
        name="shift",
    )(white)
    partial = pl.pallas_call(
        functools.partial(correlate_kernel, plan),
        out_shape=jax.ShapeDtypeStruct((source_total * (L // STEP), wide), jnp.bfloat16),
        in_specs=[VMEM, VMEM, VMEM, VMEM],
        out_specs=VMEM,
        scratch_shapes=[
            pltpu.VMEM((source_total * COARSE, DEPTH), jnp.bfloat16),
            pltpu.VMEM((wide // LANES, source_total * (L // STEP), LANES), jnp.float32),
        ],
        compiler_params=PARAMS,
        name="correlate",
    )(channel_row, near, far, shifted)
    partial, keep = lax.optimization_barrier((partial, keep))
    partial = partial.reshape(src_count, per * (L // STEP), wide)
    windows = lax.all_to_all(partial, "src", split_axis=0, concat_axis=0, tiled=True)
    stacked = jnp.sum(windows.astype(jnp.float32), axis=0)
    stacked = stacked.reshape(per, L // STEP, STEP, chan_dev).transpose(0, 3, 1, 2).reshape(per, chan_dev, L)
    factor = 1.0 / float(WL * src_count) ** 0.5
    return jnp.where(keep[:, :, None], stacked * factor, jnp.float32(0.0))


def local(record, source_channel, band_edges, offsets):
    blocks = jnp.arange(lax.axis_size("recv"), dtype=jnp.int32)
    owners = source_channel // record.shape[0]
    held = jnp.sum((owners[None, :] == blocks[:, None]).astype(jnp.int32), axis=1)
    choice = jnp.max(sum((held > plan[0]).astype(jnp.int32) for plan in PLANS[:-1]))
    return lax.switch(
        choice,
        [functools.partial(stack, plan) for plan in PLANS],
        record,
        source_channel,
        band_edges,
        offsets,
    )


def solution(mesh):
    in_specs = (P("recv", "src"), P(), P(), P())
    out_specs = P("src", "recv", None)
    return jax.shard_map(local, mesh=mesh, in_specs=in_specs, out_specs=out_specs, check_vma=False)
```

```python
import functools

import jax
import jax.numpy as jnp
from jax import lax
from jax.experimental import pallas as pl
from jax.experimental.pallas import tpu as pltpu
from jax.sharding import PartitionSpec as P

WL = 2560
L = 256
SEG = WL + L
LANES = 128
TILES = SEG // LANES
BODY = WL // LANES
STEP = 16
COARSE = LANES // STEP
DEPTH = WL + LANES
EPSILON = 1e-06
CORES = 2
PLANS = ((3, 5, 16), (4, 2, 8), (6, 4, 24), (16, 1, 16))

VMEM = pl.BlockSpec(memory_space=pltpu.VMEM)
SMEM = pl.BlockSpec(memory_space=pltpu.SMEM)
PARAMS = pltpu.CompilerParams(vmem_limit_bytes=40 * 1024 * 1024)
EARLY = 2


def iota(shape, dim):
    return lax.broadcasted_iota(jnp.int32, shape, dim)


def column(row):
    count = row.shape[1]
    square = iota((count, count), 0) == iota((count, count), 1)
    return jnp.sum(jnp.where(square, jnp.broadcast_to(row, (count, count)), 0), axis=1, keepdims=True)


def one_hot(mask):
    return jnp.where(mask, 1.0, 0.0).astype(jnp.bfloat16)


def prepare_kernel(recv_count, plans, *refs):
    offsets_hbm, channel_hbm, record_hbm, white_ref, choice_ref = refs[:5]
    send_refs = refs[5 : 5 + len(plans)]
    offsets_ref, channel_ref, record_ref, chosen_ref, sems = refs[5 + len(plans) :]
    copies = [
        pltpu.make_async_copy(offsets_hbm, offsets_ref, sems.at[0]),
        pltpu.make_async_copy(channel_hbm, channel_ref, sems.at[1]),
        pltpu.make_async_copy(record_hbm, record_ref, sems.at[2]),
    ]
    for copy in copies:
        copy.start()
    copies[1].wait()
    chan_dev = record_ref.shape[0]
    owner = jnp.broadcast_to(channel_ref[...] // chan_dev, (recv_count, channel_ref.shape[1]))
    held = jnp.sum(jnp.where(owner == iota(owner.shape, 0), 1, 0), axis=1, keepdims=True)
    most = jnp.max(held)
    chosen_ref[0] = sum((most > plan[0]).astype(jnp.int32) for plan in PLANS[:-1])
    choosing = pltpu.make_async_copy(chosen_ref, choice_ref, sems.at[3])
    choosing.start()
    copies[0].wait()
    copies[2].wait()
    start = offsets_ref[lax.axis_index("src")]
    first = start // LANES
    rest = start - first * LANES
    last = record_ref.shape[1] // LANES - 1
    lane = iota((chan_dev, LANES), 1)
    shift = lax.rem(LANES - rest, LANES)

    def rolled(tile):
        at = pl.multiple_of(jnp.minimum(first + tile, last) * LANES, LANES)
        return pltpu.roll(record_ref[:, pl.ds(at, LANES)].astype(jnp.float32), shift, 1)

    segment = []
    total = jnp.zeros((chan_dev, LANES), jnp.float32)
    left = rolled(0)
    for tile in range(TILES):
        right = rolled(tile + 1)
        piece = jnp.where(lane < LANES - rest, left, right)
        segment.append(piece)
        total = total + piece * piece
        left = right
    power = jnp.sum(total, axis=1, keepdims=True) / SEG
    spread = jnp.broadcast_to(jnp.sqrt(power + EPSILON), (chan_dev, LANES))
    for tile in range(TILES):
        white_ref[:, tile * LANES : (tile + 1) * LANES] = (segment[tile] / spread).astype(jnp.bfloat16)
    for plan, send_ref in zip(plans, send_refs, strict=True):
        pack(plan, channel_ref, white_ref, send_ref)
    choosing.wait()


def pack(plan, channel_ref, white_ref, send_ref):
    slots, split, rows = plan
    chan_dev = white_ref.shape[0]
    base = lax.axis_index("recv") * chan_dev
    source = column(channel_ref[...])
    mine = iota((source.shape[0], chan_dev), 1) + base
    is_source = jnp.sum(jnp.where(source == mine, 1, 0), axis=0, keepdims=True)
    before = jnp.sum(jnp.where((source >= base) & (source < mine), 1, 0), axis=0, keepdims=True)
    row = iota((rows, chan_dev), 0)
    width = WL // split
    packed = None
    for part in range(split):
        pick = (before == row - part * slots) & (is_source > 0) & (row >= part * slots) & (row < (part + 1) * slots)
        term = jnp.dot(
            one_hot(pick),
            white_ref[:, L // 2 + part * width : L // 2 + (part + 1) * width],
            preferred_element_type=jnp.float32,
        )
        packed = term if packed is None else packed + term
    packed = packed.astype(jnp.bfloat16)
    for dest in range(send_ref.shape[0]):
        send_ref[dest] = packed


def shift_kernel(white_ref, shifted_ref, rows_ref):
    chan_dev = white_ref.shape[0]
    white = white_ref[...]
    for l in range(STEP):
        rows_ref[l * chan_dev : (l + 1) * chan_dev, :] = pltpu.roll(white, SEG - l, 1) if l else white
    for tile in range(TILES):
        at = slice(tile * LANES, (tile + 1) * LANES)
        shifted_ref[at, :] = rows_ref[:, at].T


def correlate_kernel(plan, channel_ref, near_ref, far_ref, shifted_ref, out_ref, a_ref, part_ref):
    slots, split, rows = plan
    wide = shifted_ref.shape[1]
    chan_dev = wide // STEP
    count = channel_ref.shape[1]
    half = count // 2
    core = lax.rem(lax.axis_index("recv"), CORES)
    order = iota((count, count), 0)
    order = jnp.where(order < half, 2 * order, 2 * (order - half) + 1)
    every = jnp.broadcast_to(channel_ref[...], (count, count))
    source = jnp.sum(jnp.where(order == iota((count, count), 1), every, 0), axis=1, keepdims=True)
    owner = source // chan_dev
    place = jnp.sum(jnp.where((every >= owner * chan_dev) & (every < source), 1, 0), axis=1, keepdims=True)
    at = (owner // CORES) * rows + place
    groups = near_ref.shape[0]
    total = groups * rows
    width = WL // split
    both = jnp.concatenate([near_ref[...].reshape(total, width), far_ref[...].reshape(total, width)], axis=0)
    at = jnp.where(lax.rem(owner, CORES) == core, at, at + total)
    hits = [one_hot(iota((count, CORES * total), 1) == at + part * slots) for part in range(split)]
    gathered = jnp.dot(jnp.concatenate(hits, axis=0), both, preferred_element_type=jnp.float32).astype(jnp.bfloat16)
    pieces = [gathered[part * count : (part + 1) * count] for part in range(split)]
    joined = jnp.concatenate(pieces + [jnp.zeros((count, LANES), jnp.bfloat16)], axis=1)
    for m in range(COARSE):
        a_ref[m * count : (m + 1) * count, :] = pltpu.roll(joined, STEP * m, 1) if m else joined
    for high in range(L // LANES):
        product = jnp.dot(
            a_ref[...],
            shifted_ref[high * LANES : high * LANES + DEPTH, :],
            preferred_element_type=jnp.float32,
        )
        for low in range(COARSE):
            m = high * COARSE + low
            for j in range(2):
                row = low * count + j * half
                for n in range(wide // LANES):
                    part_ref[n, pl.ds(j * STEP + m, half, stride=2 * STEP), :] = product[
                        row : row + half, n * LANES : (n + 1) * LANES
                    ]
    for n in range(wide // LANES):
        out_ref[:, n * LANES : (n + 1) * LANES] = part_ref[n].astype(jnp.bfloat16)


def prepare(plans, record, source_channel, offsets):
    chan_dev = record.shape[0]
    recv_count = lax.axis_size("recv")
    channel_row = source_channel.reshape(1, source_channel.shape[0])
    return pl.pallas_call(
        functools.partial(prepare_kernel, recv_count, plans),
        out_shape=[
            jax.ShapeDtypeStruct((chan_dev, SEG), jnp.bfloat16),
            jax.ShapeDtypeStruct((1,), jnp.int32),
        ]
        + [
            jax.ShapeDtypeStruct((recv_count // CORES, rows, WL // split), jnp.bfloat16) for _, split, rows in plans
        ],
        in_specs=[pl.BlockSpec(memory_space=pl.ANY)] * 3,
        out_specs=[VMEM, pl.BlockSpec(memory_space=pl.ANY)] + [VMEM] * len(plans),
        scratch_shapes=[
            pltpu.SMEM(offsets.shape, jnp.int32),
            pltpu.VMEM(channel_row.shape, jnp.int32),
            pltpu.VMEM(record.shape, record.dtype),
            pltpu.SMEM((1,), jnp.int32),
            pltpu.SemaphoreType.DMA((4,)),
        ],
        compiler_params=PARAMS,
        name="prepare",
    )(offsets, channel_row, record)


def stack(number, record, source_channel, band_edges, offsets, white, *sends):
    plan = PLANS[number]
    chan_dev = white.shape[0]
    recv_index = lax.axis_index("recv")
    src_index = lax.axis_index("src")
    recv_count = lax.axis_size("recv")
    src_count = lax.axis_size("src")
    source_total = source_channel.shape[0]
    per = source_total // src_count
    wide = STEP * chan_dev
    channel_row = source_channel.reshape(1, source_total)
    if number < EARLY:
        send = sends[number]
    else:
        white, _, send = prepare([plan], record, source_channel, offsets)
    near = lax.all_to_all(
        send,
        "recv",
        split_axis=0,
        concat_axis=0,
        tiled=True,
        axis_index_groups=[list(range(core, recv_count, CORES)) for core in range(CORES)],
    )
    far = lax.ppermute(near, "recv", [(i, i ^ 1) for i in range(recv_count)])
    far, source_channel, band_edges = lax.optimization_barrier((far, source_channel, band_edges))
    own_channel = lax.dynamic_slice_in_dim(source_channel, src_index * per, per, 0)
    own_edges = lax.dynamic_slice_in_dim(band_edges, src_index * per, per, 0)
    channel_ids = recv_index * chan_dev + jnp.arange(chan_dev, dtype=jnp.int32)
    keep = (channel_ids[None, :] >= own_edges[:, 0:1]) & (channel_ids[None, :] < own_edges[:, 1:2])
    keep = keep & (channel_ids[None, :] != own_channel[:, None])
    shifted = pl.pallas_call(
        shift_kernel,
        out_shape=jax.ShapeDtypeStruct((SEG, wide), jnp.bfloat16),
        in_specs=[VMEM],
        out_specs=VMEM,
        scratch_shapes=[pltpu.VMEM((wide, SEG), jnp.bfloat16)],
        compiler_params=PARAMS,
        cost_estimate=pl.CostEstimate(flops=10**9, bytes_accessed=4 * 10**6, transcendentals=0),
        name="shift",
    )(white)
    partial = pl.pallas_call(
        functools.partial(correlate_kernel, plan),
        out_shape=jax.ShapeDtypeStruct((source_total * (L // STEP), wide), jnp.bfloat16),
        in_specs=[VMEM, VMEM, VMEM, VMEM],
        out_specs=VMEM,
        scratch_shapes=[
            pltpu.VMEM((source_total * COARSE, DEPTH), jnp.bfloat16),
            pltpu.VMEM((wide // LANES, source_total * (L // STEP), LANES), jnp.float32),
        ],
        compiler_params=PARAMS,
        name="correlate",
    )(channel_row, near, far, shifted)
    partial, keep = lax.optimization_barrier((partial, keep))
    partial = partial.reshape(src_count, per * (L // STEP), wide)
    windows = lax.all_to_all(partial, "src", split_axis=0, concat_axis=0, tiled=True)
    stacked = jnp.sum(windows.astype(jnp.float32), axis=0)
    stacked = stacked.reshape(per, L // STEP, STEP, chan_dev).transpose(0, 3, 1, 2).reshape(per, chan_dev, L)
    factor = 1.0 / float(WL * src_count) ** 0.5
    return jnp.where(keep[:, :, None], stacked * factor, jnp.float32(0.0))


def local(record, source_channel, band_edges, offsets):
    white, choice, *sends = prepare(PLANS[:EARLY], record, source_channel, offsets)
    return lax.switch(
        choice[0],
        [functools.partial(stack, number) for number in range(len(PLANS))],
        record,
        source_channel,
        band_edges,
        offsets,
        white,
        *sends,
    )


def solution(mesh):
    in_specs = (P("recv", "src"), P(), P(), P())
    out_specs = P("src", "recv", None)
    return jax.shard_map(local, mesh=mesh, in_specs=in_specs, out_specs=out_specs, check_vma=False)
```

```python
import functools

import jax
import jax.numpy as jnp
from jax import lax
from jax.experimental import pallas as pl
from jax.experimental.pallas import tpu as pltpu
from jax.sharding import PartitionSpec as P

WL = 2560
L = 256
SEG = WL + L
LANES = 128
TILES = SEG // LANES
BODY = WL // LANES
STEP = 16
COARSE = LANES // STEP
DEPTH = WL + LANES
EPSILON = 1e-06
CORES = 2
PARTNERS = 2
PLANS = ((3, 5, 16), (4, 2, 8), (6, 4, 24), (16, 1, 16))

VMEM = pl.BlockSpec(memory_space=pltpu.VMEM)
SMEM = pl.BlockSpec(memory_space=pltpu.SMEM)
PARAMS = pltpu.CompilerParams(vmem_limit_bytes=40 * 1024 * 1024)
EARLY = 2


def iota(shape, dim):
    return lax.broadcasted_iota(jnp.int32, shape, dim)


def column(row):
    count = row.shape[1]
    square = iota((count, count), 0) == iota((count, count), 1)
    return jnp.sum(jnp.where(square, jnp.broadcast_to(row, (count, count)), 0), axis=1, keepdims=True)


def one_hot(mask):
    return jnp.where(mask, 1.0, 0.0).astype(jnp.bfloat16)


def prepare_kernel(recv_count, plans, *refs):
    offsets_hbm, channel_hbm, record_hbm, white_ref, choice_ref = refs[:5]
    send_refs = refs[5 : 5 + len(plans)]
    offsets_ref, channel_ref, record_ref, chosen_ref, sems = refs[5 + len(plans) :]
    copies = [
        pltpu.make_async_copy(offsets_hbm, offsets_ref, sems.at[0]),
        pltpu.make_async_copy(channel_hbm, channel_ref, sems.at[1]),
        pltpu.make_async_copy(record_hbm, record_ref, sems.at[2]),
    ]
    for copy in copies:
        copy.start()
    copies[1].wait()
    chan_dev = record_ref.shape[0]
    owner = jnp.broadcast_to(channel_ref[...] // chan_dev, (recv_count, channel_ref.shape[1]))
    held = jnp.sum(jnp.where(owner == iota(owner.shape, 0), 1, 0), axis=1, keepdims=True)
    most = jnp.max(held)
    chosen_ref[0] = sum((most > plan[0]).astype(jnp.int32) for plan in PLANS[:-1])
    choosing = pltpu.make_async_copy(chosen_ref, choice_ref, sems.at[3])
    choosing.start()
    copies[0].wait()
    copies[2].wait()
    start = offsets_ref[lax.axis_index("src")]
    first = start // LANES
    rest = start - first * LANES
    last = record_ref.shape[1] // LANES - 1
    lane = iota((chan_dev, LANES), 1)
    shift = lax.rem(LANES - rest, LANES)

    def rolled(tile):
        at = pl.multiple_of(jnp.minimum(first + tile, last) * LANES, LANES)
        return pltpu.roll(record_ref[:, pl.ds(at, LANES)].astype(jnp.float32), shift, 1)

    segment = []
    total = jnp.zeros((chan_dev, LANES), jnp.float32)
    left = rolled(0)
    for tile in range(TILES):
        right = rolled(tile + 1)
        piece = jnp.where(lane < LANES - rest, left, right)
        segment.append(piece)
        total = total + piece * piece
        left = right
    power = jnp.sum(total, axis=1, keepdims=True) / SEG
    spread = jnp.broadcast_to(jnp.sqrt(power + EPSILON), (chan_dev, LANES))
    for tile in range(TILES):
        white_ref[:, tile * LANES : (tile + 1) * LANES] = (segment[tile] / spread).astype(jnp.bfloat16)
    for plan, send_ref in zip(plans, send_refs, strict=True):
        pack(plan, channel_ref, white_ref, send_ref)
    choosing.wait()


def pack(plan, channel_ref, white_ref, send_ref):
    slots, split, rows = plan
    chan_dev = white_ref.shape[0]
    base = lax.axis_index("recv") * chan_dev
    source = column(channel_ref[...])
    mine = iota((source.shape[0], chan_dev), 1) + base
    is_source = jnp.sum(jnp.where(source == mine, 1, 0), axis=0, keepdims=True)
    before = jnp.sum(jnp.where((source >= base) & (source < mine), 1, 0), axis=0, keepdims=True)
    row = iota((rows, chan_dev), 0)
    width = WL // split
    packed = None
    for part in range(split):
        pick = (before == row - part * slots) & (is_source > 0) & (row >= part * slots) & (row < (part + 1) * slots)
        term = jnp.dot(
            one_hot(pick),
            white_ref[:, L // 2 + part * width : L // 2 + (part + 1) * width],
            preferred_element_type=jnp.float32,
        )
        packed = term if packed is None else packed + term
    packed = packed.astype(jnp.bfloat16)
    for dest in range(send_ref.shape[0]):
        send_ref[dest] = packed


def shift_kernel(white_ref, shifted_ref, rows_ref):
    chan_dev = white_ref.shape[0]
    white = white_ref[...]
    for l in range(STEP):
        rows_ref[l * chan_dev : (l + 1) * chan_dev, :] = pltpu.roll(white, SEG - l, 1) if l else white
    for tile in range(TILES):
        at = slice(tile * LANES, (tile + 1) * LANES)
        shifted_ref[at, :] = rows_ref[:, at].T


def correlate_kernel(plan, flip, channel_ref, near_ref, far_ref, shifted_ref, out_ref, a_ref, part_ref):
    slots, split, rows = plan
    wide = shifted_ref.shape[1]
    chan_dev = wide // STEP
    total_sources = channel_ref.shape[1]
    count = total_sources // PARTNERS
    half = count // 2
    core = lax.rem(lax.axis_index("recv"), CORES)
    side = lax.rem(lax.axis_index("src") + flip, PARTNERS)
    order = iota((count, total_sources), 0)
    second = jnp.where(order < half, 0, 1)
    order = 2 * (PARTNERS * (order - half * second) + side) + second
    every = jnp.broadcast_to(channel_ref[...], (count, total_sources))
    source = jnp.sum(jnp.where(order == iota((count, total_sources), 1), every, 0), axis=1, keepdims=True)
    owner = source // chan_dev
    place = jnp.sum(jnp.where((every >= owner * chan_dev) & (every < source), 1, 0), axis=1, keepdims=True)
    at = (owner // CORES) * rows + place
    groups = near_ref.shape[0]
    total = groups * rows
    width = WL // split
    both = jnp.concatenate([near_ref[...].reshape(total, width), far_ref[...].reshape(total, width)], axis=0)
    at = jnp.where(lax.rem(owner, CORES) == core, at, at + total)
    hits = [one_hot(iota((count, CORES * total), 1) == at + part * slots) for part in range(split)]
    gathered = jnp.dot(jnp.concatenate(hits, axis=0), both, preferred_element_type=jnp.float32).astype(jnp.bfloat16)
    pieces = [gathered[part * count : (part + 1) * count] for part in range(split)]
    joined = jnp.concatenate(pieces + [jnp.zeros((count, LANES), jnp.bfloat16)], axis=1)
    for m in range(COARSE):
        a_ref[m * count : (m + 1) * count, :] = pltpu.roll(joined, STEP * m, 1) if m else joined
    for high in range(L // LANES):
        product = jnp.dot(
            a_ref[...],
            shifted_ref[high * LANES : high * LANES + DEPTH, :],
            preferred_element_type=jnp.float32,
        )
        for low in range(COARSE):
            m = high * COARSE + low
            for j in range(2):
                row = low * count + j * half
                for n in range(wide // LANES):
                    part_ref[n, pl.ds(j * STEP + m, half, stride=2 * STEP), :] = product[
                        row : row + half, n * LANES : (n + 1) * LANES
                    ]
    for n in range(wide // LANES):
        out_ref[:, n * LANES : (n + 1) * LANES] = part_ref[n].astype(out_ref.dtype)


def prepare(plans, record, source_channel, offsets):
    chan_dev = record.shape[0]
    recv_count = lax.axis_size("recv")
    channel_row = source_channel.reshape(1, source_channel.shape[0])
    return pl.pallas_call(
        functools.partial(prepare_kernel, recv_count, plans),
        out_shape=[
            jax.ShapeDtypeStruct((chan_dev, SEG), jnp.bfloat16),
            jax.ShapeDtypeStruct((1,), jnp.int32),
        ]
        + [
            jax.ShapeDtypeStruct((recv_count // CORES, rows, WL // split), jnp.bfloat16) for _, split, rows in plans
        ],
        in_specs=[pl.BlockSpec(memory_space=pl.ANY)] * 3,
        out_specs=[VMEM, pl.BlockSpec(memory_space=pl.ANY)] + [VMEM] * len(plans),
        scratch_shapes=[
            pltpu.SMEM(offsets.shape, jnp.int32),
            pltpu.VMEM(channel_row.shape, jnp.int32),
            pltpu.VMEM(record.shape, record.dtype),
            pltpu.SMEM((1,), jnp.int32),
            pltpu.SemaphoreType.DMA((4,)),
        ],
        compiler_params=PARAMS,
        name="prepare",
    )(offsets, channel_row, record)


def stack(number, record, source_channel, band_edges, offsets, white, *sends):
    plan = PLANS[number]
    chan_dev = white.shape[0]
    recv_index = lax.axis_index("recv")
    src_index = lax.axis_index("src")
    recv_count = lax.axis_size("recv")
    src_count = lax.axis_size("src")
    source_total = source_channel.shape[0]
    per = source_total // src_count
    wide = STEP * chan_dev
    channel_row = source_channel.reshape(1, source_total)
    if number < EARLY:
        send = sends[number]
    else:
        white, _, send = prepare([plan], record, source_channel, offsets)
    near = lax.all_to_all(
        send,
        "recv",
        split_axis=0,
        concat_axis=0,
        tiled=True,
        axis_index_groups=[list(range(core, recv_count, CORES)) for core in range(CORES)],
    )
    far = lax.ppermute(near, "recv", [(i, i ^ 1) for i in range(recv_count)])
    shifted = pl.pallas_call(
        shift_kernel,
        out_shape=jax.ShapeDtypeStruct((SEG, wide), jnp.bfloat16),
        in_specs=[VMEM],
        out_specs=VMEM,
        scratch_shapes=[pltpu.VMEM((wide, SEG), jnp.bfloat16)],
        compiler_params=PARAMS,
        cost_estimate=pl.CostEstimate(flops=10**9, bytes_accessed=4 * 10**6, transcendentals=0),
        name="shift",
    )(white)
    deep = per * (L // STEP)
    results = source_total // PARTNERS * (L // STEP)

    def correlate(flip, dtype, name):
        return pl.pallas_call(
            functools.partial(correlate_kernel, plan, flip),
            out_shape=jax.ShapeDtypeStruct((results, wide), dtype),
            in_specs=[VMEM, VMEM, VMEM, VMEM],
            out_specs=VMEM,
            scratch_shapes=[
                pltpu.VMEM((source_total // PARTNERS * COARSE, DEPTH), jnp.bfloat16),
                pltpu.VMEM((wide // LANES, results, LANES), jnp.float32),
            ],
            compiler_params=PARAMS,
            cost_estimate=pl.CostEstimate(flops=10**9, bytes_accessed=4 * 10**6, transcendentals=0),
            name=name,
        )(channel_row, near, far, shifted)

    away = correlate(1, jnp.bfloat16, "away")
    away, near, source_channel, band_edges = lax.optimization_barrier((away, near, source_channel, band_edges))
    came = lax.ppermute(away, "src", [(i, i ^ 1) for i in range(src_count)])
    home = correlate(0, jnp.float32, "home")
    own_channel = lax.dynamic_slice_in_dim(source_channel, src_index * per, per, 0)
    own_edges = lax.dynamic_slice_in_dim(band_edges, src_index * per, per, 0)
    channel_ids = recv_index * chan_dev + jnp.arange(chan_dev, dtype=jnp.int32)
    keep = (channel_ids[None, :] >= own_edges[:, 0:1]) & (channel_ids[None, :] < own_edges[:, 1:2])
    keep = keep & (channel_ids[None, :] != own_channel[:, None])
    home, keep = lax.optimization_barrier((home, keep))
    partial = (home + came.astype(jnp.float32)).astype(jnp.bfloat16)
    windows = lax.all_to_all(
        partial.reshape(src_count // PARTNERS, deep, wide),
        "src",
        split_axis=0,
        concat_axis=0,
        tiled=True,
        axis_index_groups=[list(range(side, src_count, PARTNERS)) for side in range(PARTNERS)],
    )
    stacked = jnp.sum(windows.astype(jnp.float32), axis=0)
    stacked = stacked.reshape(per, L // STEP, STEP, chan_dev).transpose(0, 3, 1, 2).reshape(per, chan_dev, L)
    factor = 1.0 / float(WL * src_count) ** 0.5
    return jnp.where(keep[:, :, None], stacked * factor, jnp.float32(0.0))


def local(record, source_channel, band_edges, offsets):
    white, choice, *sends = prepare(PLANS[:EARLY], record, source_channel, offsets)
    return lax.switch(
        choice[0],
        [functools.partial(stack, number) for number in range(len(PLANS))],
        record,
        source_channel,
        band_edges,
        offsets,
        white,
        *sends,
    )


def solution(mesh):
    in_specs = (P("recv", "src"), P(), P(), P())
    out_specs = P("src", "recv", None)
    return jax.shard_map(local, mesh=mesh, in_specs=in_specs, out_specs=out_specs, check_vma=False)
```

```python
import functools

import jax
import jax.numpy as jnp
from jax import lax
from jax.experimental import pallas as pl
from jax.experimental.pallas import tpu as pltpu
from jax.sharding import PartitionSpec as P

WL = 2560
L = 256
SEG = WL + L
LANES = 128
TILES = SEG // LANES
BODY = WL // LANES
STEP = 16
COARSE = LANES // STEP
DEPTH = WL + LANES
EPSILON = 1e-06
CORES = 2
PARTNERS = 2
PLANS = ((3, 5, 16), (4, 2, 8), (6, 4, 24), (16, 1, 16))

VMEM = pl.BlockSpec(memory_space=pltpu.VMEM)
SMEM = pl.BlockSpec(memory_space=pltpu.SMEM)
PARAMS = pltpu.CompilerParams(vmem_limit_bytes=40 * 1024 * 1024)
EARLY = 2


def iota(shape, dim):
    return lax.broadcasted_iota(jnp.int32, shape, dim)


def column(row):
    count = row.shape[1]
    square = iota((count, count), 0) == iota((count, count), 1)
    return jnp.sum(jnp.where(square, jnp.broadcast_to(row, (count, count)), 0), axis=1, keepdims=True)


def one_hot(mask):
    return jnp.where(mask, 1.0, 0.0).astype(jnp.bfloat16)


def prepare_kernel(recv_count, plans, *refs):
    offsets_hbm, channel_hbm, record_hbm, white_ref, choice_ref = refs[:5]
    send_refs = refs[5 : 5 + len(plans)]
    offsets_ref, channel_ref, record_ref, chosen_ref, sems = refs[5 + len(plans) :]
    copies = [
        pltpu.make_async_copy(offsets_hbm, offsets_ref, sems.at[0]),
        pltpu.make_async_copy(channel_hbm, channel_ref, sems.at[1]),
        pltpu.make_async_copy(record_hbm, record_ref, sems.at[2]),
    ]
    for copy in copies:
        copy.start()
    copies[1].wait()
    chan_dev = record_ref.shape[0]
    owner = jnp.broadcast_to(channel_ref[...] // chan_dev, (recv_count, channel_ref.shape[1]))
    held = jnp.sum(jnp.where(owner == iota(owner.shape, 0), 1, 0), axis=1, keepdims=True)
    most = jnp.max(held)
    chosen_ref[0] = sum((most > plan[0]).astype(jnp.int32) for plan in PLANS[:-1])
    choosing = pltpu.make_async_copy(chosen_ref, choice_ref, sems.at[3])
    choosing.start()
    copies[0].wait()
    copies[2].wait()
    start = offsets_ref[lax.axis_index("src")]
    first = start // LANES
    rest = start - first * LANES
    last = record_ref.shape[1] // LANES - 1
    lane = iota((chan_dev, LANES), 1)
    shift = lax.rem(LANES - rest, LANES)

    def rolled(tile):
        at = pl.multiple_of(jnp.minimum(first + tile, last) * LANES, LANES)
        return pltpu.roll(record_ref[:, pl.ds(at, LANES)].astype(jnp.float32), shift, 1)

    segment = []
    total = jnp.zeros((chan_dev, LANES), jnp.float32)
    left = rolled(0)
    for tile in range(TILES):
        right = rolled(tile + 1)
        piece = jnp.where(lane < LANES - rest, left, right)
        segment.append(piece)
        total = total + piece * piece
        left = right
    power = jnp.sum(total, axis=1, keepdims=True) / SEG
    spread = jnp.broadcast_to(jnp.sqrt(power + EPSILON), (chan_dev, LANES))
    for tile in range(TILES):
        white_ref[:, tile * LANES : (tile + 1) * LANES] = (segment[tile] / spread).astype(jnp.bfloat16)
    for plan, send_ref in zip(plans, send_refs, strict=True):
        pack(plan, channel_ref, white_ref, send_ref)
    choosing.wait()


def pack(plan, channel_ref, white_ref, send_ref):
    slots, split, rows = plan
    chan_dev = white_ref.shape[0]
    base = lax.axis_index("recv") * chan_dev
    source = column(channel_ref[...])
    mine = iota((source.shape[0], chan_dev), 1) + base
    is_source = jnp.sum(jnp.where(source == mine, 1, 0), axis=0, keepdims=True)
    before = jnp.sum(jnp.where((source >= base) & (source < mine), 1, 0), axis=0, keepdims=True)
    row = iota((rows, chan_dev), 0)
    width = WL // split
    packed = None
    for part in range(split):
        pick = (before == row - part * slots) & (is_source > 0) & (row >= part * slots) & (row < (part + 1) * slots)
        term = jnp.dot(
            one_hot(pick),
            white_ref[:, L // 2 + part * width : L // 2 + (part + 1) * width],
            preferred_element_type=jnp.float32,
        )
        packed = term if packed is None else packed + term
    packed = packed.astype(jnp.bfloat16)
    for dest in range(send_ref.shape[0]):
        send_ref[dest] = packed


def shift_kernel(white_ref, shifted_ref, rows_ref):
    chan_dev = white_ref.shape[0]
    white = white_ref[...]
    for l in range(STEP):
        rows_ref[l * chan_dev : (l + 1) * chan_dev, :] = pltpu.roll(white, SEG - l, 1) if l else white
    for tile in range(TILES):
        at = slice(tile * LANES, (tile + 1) * LANES)
        shifted_ref[at, :] = rows_ref[:, at].T


def correlate_kernel(plan, flip, channel_ref, near_ref, far_ref, shifted_ref, out_ref, a_ref, part_ref):
    slots, split, rows = plan
    wide = shifted_ref.shape[1]
    chan_dev = wide // STEP
    total_sources = channel_ref.shape[1]
    count = total_sources // PARTNERS
    half = count // 2
    core = lax.rem(lax.axis_index("recv"), CORES)
    side = lax.rem(lax.axis_index("src") + flip, PARTNERS)
    order = iota((count, total_sources), 0)
    second = jnp.where(order < half, 0, 1)
    order = 2 * (PARTNERS * (order - half * second) + side) + second
    every = jnp.broadcast_to(channel_ref[...], (count, total_sources))
    source = jnp.sum(jnp.where(order == iota((count, total_sources), 1), every, 0), axis=1, keepdims=True)
    owner = source // chan_dev
    place = jnp.sum(jnp.where((every >= owner * chan_dev) & (every < source), 1, 0), axis=1, keepdims=True)
    at = (owner // CORES) * rows + place
    groups = near_ref.shape[0]
    total = groups * rows
    width = WL // split
    both = jnp.concatenate([near_ref[...].reshape(total, width), far_ref[...].reshape(total, width)], axis=0)
    at = jnp.where(lax.rem(owner, CORES) == core, at, at + total)
    hits = [one_hot(iota((count, CORES * total), 1) == at + part * slots) for part in range(split)]
    gathered = jnp.dot(jnp.concatenate(hits, axis=0), both, preferred_element_type=jnp.float32).astype(jnp.bfloat16)
    pieces = [gathered[part * count : (part + 1) * count] for part in range(split)]
    joined = jnp.concatenate(pieces + [jnp.zeros((count, LANES), jnp.bfloat16)], axis=1)
    for m in range(COARSE):
        a_ref[m * count : (m + 1) * count, :] = pltpu.roll(joined, STEP * m, 1) if m else joined
    for high in range(L // LANES):
        product = jnp.dot(
            a_ref[...],
            shifted_ref[high * LANES : high * LANES + DEPTH, :],
            preferred_element_type=jnp.float32,
        )
        for low in range(COARSE):
            m = high * COARSE + low
            for j in range(2):
                row = low * count + j * half
                for n in range(wide // LANES):
                    part_ref[n, pl.ds(j * STEP + m, half, stride=2 * STEP), :] = product[
                        row : row + half, n * LANES : (n + 1) * LANES
                    ]
    for n in range(wide // LANES):
        out_ref[:, n * LANES : (n + 1) * LANES] = part_ref[n].astype(out_ref.dtype)


def prepare(plans, record, source_channel, offsets):
    chan_dev = record.shape[0]
    recv_count = lax.axis_size("recv")
    channel_row = source_channel.reshape(1, source_channel.shape[0])
    return pl.pallas_call(
        functools.partial(prepare_kernel, recv_count, plans),
        out_shape=[
            jax.ShapeDtypeStruct((chan_dev, SEG), jnp.bfloat16),
            jax.ShapeDtypeStruct((1,), jnp.int32),
        ]
        + [
            jax.ShapeDtypeStruct((recv_count // CORES, rows, WL // split), jnp.bfloat16) for _, split, rows in plans
        ],
        in_specs=[pl.BlockSpec(memory_space=pl.ANY)] * 3,
        out_specs=[VMEM, pl.BlockSpec(memory_space=pl.ANY)] + [VMEM] * len(plans),
        scratch_shapes=[
            pltpu.SMEM(offsets.shape, jnp.int32),
            pltpu.VMEM(channel_row.shape, jnp.int32),
            pltpu.VMEM(record.shape, record.dtype),
            pltpu.SMEM((1,), jnp.int32),
            pltpu.SemaphoreType.DMA((4,)),
        ],
        compiler_params=PARAMS,
        name="prepare",
    )(offsets, channel_row, record)


def stack(number, record, source_channel, band_edges, offsets, white, *sends):
    plan = PLANS[number]
    chan_dev = white.shape[0]
    recv_index = lax.axis_index("recv")
    src_index = lax.axis_index("src")
    recv_count = lax.axis_size("recv")
    src_count = lax.axis_size("src")
    source_total = source_channel.shape[0]
    per = source_total // src_count
    wide = STEP * chan_dev
    channel_row = source_channel.reshape(1, source_total)
    if number < EARLY:
        send = sends[number]
    else:
        white, _, send = prepare([plan], record, source_channel, offsets)
    near = lax.all_to_all(
        send,
        "recv",
        split_axis=0,
        concat_axis=0,
        tiled=True,
        axis_index_groups=[list(range(core, recv_count, CORES)) for core in range(CORES)],
    )
    far = lax.ppermute(near, "recv", [(i, i ^ 1) for i in range(recv_count)])
    shifted = pl.pallas_call(
        shift_kernel,
        out_shape=jax.ShapeDtypeStruct((SEG, wide), jnp.bfloat16),
        in_specs=[VMEM],
        out_specs=VMEM,
        scratch_shapes=[pltpu.VMEM((wide, SEG), jnp.bfloat16)],
        compiler_params=PARAMS,
        cost_estimate=pl.CostEstimate(flops=10**9, bytes_accessed=4 * 10**6, transcendentals=0),
        name="shift",
    )(white)
    deep = per * (L // STEP)
    results = source_total // PARTNERS * (L // STEP)

    def correlate(flip, dtype, name):
        return pl.pallas_call(
            functools.partial(correlate_kernel, plan, flip),
            out_shape=jax.ShapeDtypeStruct((results, wide), dtype),
            in_specs=[VMEM, VMEM, VMEM, VMEM],
            out_specs=VMEM,
            scratch_shapes=[
                pltpu.VMEM((source_total // PARTNERS * COARSE, DEPTH), jnp.bfloat16),
                pltpu.VMEM((wide // LANES, results, LANES), jnp.float32),
            ],
            compiler_params=PARAMS,
            cost_estimate=pl.CostEstimate(flops=10**9, bytes_accessed=4 * 10**6, transcendentals=0),
            name=name,
        )(channel_row, near, far, shifted)

    away = correlate(1, jnp.bfloat16, "away")
    away, near, source_channel, band_edges, src_index = lax.optimization_barrier(
        (away, near, source_channel, band_edges, src_index)
    )
    came = lax.ppermute(away, "src", [(i, i ^ 1) for i in range(src_count)])
    home = correlate(0, jnp.float32, "home")
    own = src_index * per + jnp.arange(per, dtype=jnp.int32)
    own = own[:, None] == jnp.arange(source_total, dtype=jnp.int32)[None, :]
    channel_ids = recv_index * chan_dev + jnp.arange(chan_dev, dtype=jnp.int32)
    inside = (channel_ids[None, :] >= band_edges[:, 0:1]) & (channel_ids[None, :] < band_edges[:, 1:2])
    inside = inside & (channel_ids[None, :] != source_channel[:, None])
    keep = jnp.any(own[:, :, None] & inside[None, :, :], axis=1)
    home, keep = lax.optimization_barrier((home, keep))
    partial = (home + came.astype(jnp.float32)).astype(jnp.bfloat16)
    windows = lax.all_to_all(
        partial.reshape(src_count // PARTNERS, deep, wide),
        "src",
        split_axis=0,
        concat_axis=0,
        tiled=True,
        axis_index_groups=[list(range(side, src_count, PARTNERS)) for side in range(PARTNERS)],
    )
    stacked = jnp.sum(windows.astype(jnp.float32), axis=0)
    stacked = stacked.reshape(per, L // STEP, STEP, chan_dev).transpose(0, 3, 1, 2).reshape(per, chan_dev, L)
    factor = 1.0 / float(WL * src_count) ** 0.5
    return jnp.where(keep[:, :, None], stacked * factor, jnp.float32(0.0))


def local(record, source_channel, band_edges, offsets):
    white, choice, *sends = prepare(PLANS[:EARLY], record, source_channel, offsets)
    return lax.switch(
        choice[0],
        [functools.partial(stack, number) for number in range(len(PLANS))],
        record,
        source_channel,
        band_edges,
        offsets,
        white,
        *sends,
    )


def solution(mesh):
    in_specs = (P("recv", "src"), P(), P(), P())
    out_specs = P("src", "recv", None)
    return jax.shard_map(local, mesh=mesh, in_specs=in_specs, out_specs=out_specs, check_vma=False)
```
